256 devices in a mesh: head: 8 (over x, core), seq: 32 (over z, y).
Axes of the slice: x: 4, y: 4, z: 8, core: 2. Of those that a mesh axis runs over, the one named last changes fastest.
Arguments:
- tokens: bfloat16 [4, 16, 2048], P(None, None, 'seq'), may hold values from -16 to 16
- attn_in_weight: bfloat16 [3, 2048, 2048], P(None, 'seq', 'head'), may hold values from -0.125 to 0.125
- attn_out_weight: bfloat16 [2048, 2048], P('head', 'seq'), may hold values from -0.125 to 0.125
- ffn_in_weight: bfloat16 [2, 2048, 8192], P(None, 'seq', 'head'), may hold values from -0.125 to 0.125
- ffn_out_weight: bfloat16 [8192, 2048], P('head', 'seq'), may hold values from -0.0625 to 0.0625
- cache_keys: bfloat16 [16, 16384, 2048], P(None, 'seq', 'head'), may hold values from -60 to 60
- cache_values: bfloat16 [16, 16384, 2048], P(None, 'seq', 'head'), may hold values from -10 to 10
- lengths: int32 [16], replicated, may hold values from 1 to 16384, as said below
Outputs:
- attn_branch: bfloat16 [4, 16, 2048], P(None, None, 'seq')
- mlp_branch: bfloat16 [4, 16, 2048], P(None, None, 'seq')
The draws below stay inside these ranges and needn't reach their ends.
Inputs may be any that keep to these rules, and one draw needn't show every extreme that they name: `lengths`: some request has exactly 16384 filled positions.
All inputs are finite; a program needn't handle non-finite values.
Results may differ from the reference program's by a relative error of at most 0.013.
The reference program's roundings to bfloat16 on the way count: a program that leaves them out, or rounds other values in their place, can miss the bound.
Values may be sent and summed in bfloat16 or wider, within the bound.
No kernel may reach another device: no remote copies, remote signals or barrier semaphores. Data moves between devices by JAX's collectives and lax.ppermute only.
A program may use at most 64 MiB of HBM per device.

```python
import math
import jax
import jax.numpy as jnp
from jax import lax

D = 2048
H = 16
HD = 128
FF = 8192
STEPS = 4
REQUEST_TOTAL = 16
CACHE_DEV = 512
MAX_CACHE_LENGTH = 16384


def logarithmic_uniform(key, shape, low_end, high_end):
    return jnp.exp(jax.random.uniform(key, shape, jnp.float32, math.log(low_end), math.log(high_end)))


def draw_tokens(key, part):
    key_baseline, key_rows, key_cols = jax.random.split(key, 3)
    base = jax.random.normal(key_baseline, (STEPS, REQUEST_TOTAL, D), jnp.float32)
    column = jnp.arange(D, dtype=jnp.float32) / D
    row_scale = logarithmic_uniform(key_rows, (STEPS, REQUEST_TOTAL, 1), 0.5, 2.0)
    col_scale = jnp.exp(math.log(3.0) * column) * logarithmic_uniform(key_cols, (D,), 0.6, 1.6)
    return jnp.clip(base * row_scale * col_scale, -16.0, 16.0).astype(jnp.bfloat16)


def draw_cache_keys(key, part):
    key_baseline, key_multiplier = jax.random.split(key, 2)
    base = jax.random.normal(key_baseline, (REQUEST_TOTAL, MAX_CACHE_LENGTH, H * HD), jnp.float32)
    scale_multiplier = logarithmic_uniform(key_multiplier, (REQUEST_TOTAL, MAX_CACHE_LENGTH, 1), 0.7, 2.8)
    return jnp.clip(base * scale_multiplier, -60.0, 60.0).astype(jnp.bfloat16)


def draw_cache_values(key, part):
    key_baseline, key_offset = jax.random.split(key, 2)
    base = jax.random.normal(key_baseline, (REQUEST_TOTAL, MAX_CACHE_LENGTH, H * HD), jnp.float32)
    offsets = jax.random.uniform(key_offset, (REQUEST_TOTAL, MAX_CACHE_LENGTH // 64, 1, H * HD), jnp.float32, -1.5, 1.5)
    spread_out = jnp.broadcast_to(offsets, (REQUEST_TOTAL, MAX_CACHE_LENGTH // 64, 64, H * HD)).reshape(REQUEST_TOTAL, MAX_CACHE_LENGTH, H * HD)
    return jnp.clip(base + spread_out, -10.0, 10.0).astype(jnp.bfloat16)


def draw_lengths(key, part):
    key_len, key_pick = jax.random.split(jax.random.fold_in(key, 17), 2)
    drawn = jax.random.randint(key_len, (REQUEST_TOTAL,), 1, MAX_CACHE_LENGTH + 1)
    chosen = jax.random.randint(key_pick, (), 0, REQUEST_TOTAL)
    return jnp.where(jnp.arange(REQUEST_TOTAL, dtype=jnp.int32) == chosen, MAX_CACHE_LENGTH, drawn).astype(jnp.int32)


def block_levels(stream_key, dims, pieces, least, high):
    def one(dim, parts):
        heights = jax.random.uniform(jax.random.fold_in(jax.random.fold_in(stream_key, 6), dim), (parts,), jnp.float32, least / len(pieces), high / len(pieces))
        return jnp.repeat(jnp.exp(heights), dims[dim] // parts).reshape((-1,) + (1,) * (len(dims) - dim - 1))

    gain = one(*pieces[0])
    for cut in pieces[1:]:
        gain = gain * one(*cut)
    return gain


def centred(stream_key, dims, deviation, most, cuts=(), held_as=jnp.bfloat16):
    level = block_levels(stream_key, dims, cuts, -0.22, 0.18) if cuts else 1.0
    entries = jax.random.normal(stream_key, dims, jnp.float32) * deviation * level
    return jnp.minimum(jnp.maximum(entries, -most), most).astype(held_as)


def setup_inputs(seed: int = 0) -> dict:
    streams_of = jax.random.split(jax.random.key(seed), 9)
    tokens = draw_tokens(jax.random.fold_in(streams_of[8], 71), 0)
    attn_in_weight = centred(streams_of[1], (3, D, H * HD), D ** -0.5, 0.125, ((1, 32), (2, 8)))
    attn_out_weight = centred(streams_of[2], (H * HD, D), (H * HD) ** -0.5, 0.125, ((0, 8), (1, 32)))
    ffn_in_weight = centred(streams_of[3], (2, D, FF), D ** -0.5, 0.125, ((1, 32), (2, 8)))
    ffn_out_weight = centred(streams_of[4], (FF, D), FF ** -0.5, 0.0625, ((0, 8), (1, 32)))
    cache_keys = draw_cache_keys(jax.random.fold_in(streams_of[8], 71), 0)
    cache_values = draw_cache_values(jax.random.fold_in(streams_of[8], 71), 0)
    lengths = draw_lengths(jax.random.fold_in(streams_of[8], 71), 0)
    return dict(tokens=tokens, attn_in_weight=attn_in_weight, attn_out_weight=attn_out_weight, ffn_in_weight=ffn_in_weight, ffn_out_weight=ffn_out_weight, cache_keys=cache_keys, cache_values=cache_values, lengths=lengths)


NORM_EPSILON = 1e-05
NEG_FILL = -1e+30

def layer_norm(values):
    center = lax.optimization_barrier(jnp.mean(values, axis=-1, keepdims=True))
    deviate = values - center
    spread = lax.optimization_barrier(jnp.mean(deviate * deviate, axis=-1, keepdims=True))
    return deviate * lax.rsqrt(spread + NORM_EPSILON)

def rotate_pairs(values, positions):
    half_dim = values.shape[-1] // 2
    inverse_freq = 10000.0 ** (-2.0 * jnp.arange(half_dim, dtype=jnp.float32) / values.shape[-1])
    angles = positions.astype(jnp.float32)[:, None, None] * inverse_freq[None, None, :]
    cosine = jnp.cos(angles)
    sine = jnp.sin(angles)
    first_half = values[..., :half_dim]
    second_half = values[..., half_dim:]
    return jnp.concatenate([first_half * cosine - second_half * sine, second_half * cosine + first_half * sine], axis=-1)

def reference(tokens, attn_in_weight, attn_out_weight, ffn_in_weight, ffn_out_weight, cache_keys, cache_values, lengths):
    row_count = STEPS * REQUEST_TOTAL
    inputs = tokens.reshape(row_count, D).astype(jnp.float32)
    normed = layer_norm(inputs).astype(jnp.bfloat16)
    projected = [jnp.dot(normed, attn_in_weight[index], preferred_element_type=jnp.float32) for index in range(3)]
    positions = (lengths[None, :] + jnp.arange(STEPS, dtype=jnp.int32)[:, None]).reshape(row_count)
    query = rotate_pairs(projected[0].reshape(row_count, H, HD), positions).astype(jnp.bfloat16)
    new_keys = rotate_pairs(projected[1].reshape(row_count, H, HD), positions).astype(jnp.bfloat16)
    new_values = projected[2].reshape(row_count, H, HD).astype(jnp.bfloat16)
    query = query.reshape(STEPS, REQUEST_TOTAL, H, HD).astype(jnp.float32)
    new_keys = new_keys.reshape(STEPS, REQUEST_TOTAL, H, HD).astype(jnp.float32)
    new_values = new_values.reshape(STEPS, REQUEST_TOTAL, H, HD).astype(jnp.float32)
    score_scale = 1.0 / HD ** 0.5
    block_count = MAX_CACHE_LENGTH // CACHE_DEV

    def one_block(block_index):
        first_pos = block_index * CACHE_DEV
        key_block = lax.dynamic_slice_in_dim(cache_keys, first_pos, CACHE_DEV, 1).reshape(REQUEST_TOTAL, CACHE_DEV, H, HD)
        value_block = lax.dynamic_slice_in_dim(cache_values, first_pos, CACHE_DEV, 1).reshape(REQUEST_TOTAL, CACHE_DEV, H, HD)
        scores = jnp.einsum('trhd,rchd->rthc', query, key_block.astype(jnp.float32)) * score_scale
        places = first_pos + jnp.arange(CACHE_DEV, dtype=jnp.int32)
        valid = (places[None, :] < lengths[:, None])[:, None, None, :]
        block_top = lax.optimization_barrier(jnp.max(jnp.where(valid, scores, NEG_FILL), axis=-1))
        weights = jnp.where(valid, jnp.exp(scores - block_top[..., None]), 0.0)
        block_total = lax.optimization_barrier(jnp.sum(weights, axis=-1))
        weights_bf = weights.astype(jnp.bfloat16).astype(jnp.float32)
        block_acc = jnp.einsum('rthc,rchd->rthd', weights_bf, value_block.astype(jnp.float32))
        return (block_top, block_total, block_acc)
    tops, totals, accs = lax.map(one_block, jnp.arange(block_count, dtype=jnp.int32))
    new_scores = jnp.einsum('trhd,urhd->rthu', query, new_keys) * score_scale
    causal = (jnp.arange(STEPS)[:, None] >= jnp.arange(STEPS)[None, :])[None, :, None, :]
    new_top = lax.optimization_barrier(jnp.max(jnp.where(causal, new_scores, NEG_FILL), axis=-1))
    new_weights = jnp.where(causal, jnp.exp(new_scores - new_top[..., None]), 0.0)
    new_total = lax.optimization_barrier(jnp.sum(new_weights, axis=-1))
    new_acc = jnp.einsum('rthu,urhd->rthd', new_weights.astype(jnp.bfloat16).astype(jnp.float32), new_values)
    overall = jnp.maximum(lax.optimization_barrier(jnp.max(tops, axis=0)), new_top)
    factors = jnp.exp(tops - overall[None])
    new_factor = jnp.exp(new_top - overall)
    numer = lax.optimization_barrier(jnp.sum(factors[..., None] * accs, axis=0)) + new_factor[..., None] * new_acc
    denom = lax.optimization_barrier(jnp.sum(factors * totals, axis=0)) + new_factor * new_total
    attended = (numer / denom[..., None]).transpose(1, 0, 2, 3).reshape(row_count, H * HD).astype(jnp.bfloat16)
    branch = jnp.dot(attended, attn_out_weight, preferred_element_type=jnp.float32)
    resid = inputs + branch
    normed_two = layer_norm(resid).astype(jnp.bfloat16)
    gate = jnp.dot(normed_two, ffn_in_weight[0], preferred_element_type=jnp.float32)
    upward = jnp.dot(normed_two, ffn_in_weight[1], preferred_element_type=jnp.float32)
    hidden = (jax.nn.silu(gate) * upward).astype(jnp.bfloat16)
    mlp_out = jnp.dot(hidden, ffn_out_weight, preferred_element_type=jnp.float32)
    attn_branch = branch.astype(jnp.bfloat16).reshape(STEPS, REQUEST_TOTAL, D)
    mlp_branch = mlp_out.astype(jnp.bfloat16).reshape(STEPS, REQUEST_TOTAL, D)
    return (attn_branch, mlp_branch)
```

```python
import functools

import numpy as np
import jax
import jax.numpy as jnp
from jax import lax
from jax.experimental import pallas as pl
from jax.experimental.pallas import tpu as pltpu
from jax.sharding import PartitionSpec as P

D = 2048
HD = 128
EPS = 1e-05
NEG = -1e30
SCALE = 1.0 / HD**0.5
F32 = jnp.float32
BF = jnp.bfloat16
NT = (((1,), (1,)), ((), ()))
TN = (((0,), (0,)), ((), ()))
VM = pl.BlockSpec(memory_space=pltpu.VMEM)
PARAMS = pltpu.CompilerParams(vmem_limit_bytes=16 << 20)


def iota(shape, axis):
    return lax.broadcasted_iota(jnp.int32, shape, axis)


def mm(a, b, dims=(((1,), (0,)), ((), ()))):
    return lax.dot_general(a, b, dims, preferred_element_type=F32)


def one_hot(cond):
    return jnp.where(cond, 1.0, 0.0).astype(BF)


def to_request_major():
    n, m = iota((64, 64), 0), iota((64, 64), 1)
    return one_hot(m == (n & 3) * 16 + (n >> 2))


def to_step_major():
    m, n = iota((64, 64), 0), iota((64, 64), 1)
    return one_hot(n == (m & 15) * 4 + (m >> 4))


def split(v):
    hi = v.astype(BF).astype(F32)
    return jnp.concatenate([hi, v - hi], axis=1)


def qkv_kernel(x_ref, w_ref, out_ref):
    xp = mm(to_request_major(), x_ref[...])
    center = jnp.mean(xp, axis=1, keepdims=True)
    dev = xp - center
    spread = jnp.sum(dev * dev, axis=1, keepdims=True)
    rows = jnp.concatenate([xp, jnp.ones((16, 64), F32)], axis=0).astype(BF)
    lane, row = iota((64, 128), 1), iota((64, 128), 0)
    placed = jnp.where(lane == (row & 3), center, 0.0) + jnp.where(lane == 4 + (row & 3), spread, 0.0)
    pick = jnp.where(iota((16, 64), 0) == (iota((16, 64), 1) >> 2), 1.0, 0.0)
    stats = lax.dot_general(
        pick, placed, (((1,), (0,)), ((), ())), precision=lax.Precision.HIGHEST, preferred_element_type=F32
    )
    for k in range(3):
        part = mm(rows, w_ref[k])
        for p in range(2):
            cols = part[:, p * 128 : (p + 1) * 128]
            for r in range(16):
                out_ref[2 * r + p, :, k * 128 : (k + 1) * 128] = cols[4 * r : 4 * r + 4]
                out_ref[2 * r + p, k : k + 1, 384:512] = cols[64:65]
    for r in range(16):
        for p in range(2):
            out_ref[2 * r + p, 3:4, 384:512] = stats[r : r + 1]


def rope_kernel(got_ref, cos_ref, sin_ref, q_ref, new_ref):
    total = jnp.sum(got_ref[...], axis=0)
    stats = jnp.concatenate([got_ref[i, 3:4, 384:512] for i in range(32)], axis=0)
    center = jnp.sum(stats, axis=0, keepdims=True) * (1.0 / 32)
    dev = stats - center
    between = jnp.sum(dev * dev, axis=0, keepdims=True) * 64.0
    within = jnp.sum(stats, axis=0, keepdims=True)
    lane, row = iota((4, 128), 1), iota((4, 128), 0)
    mean = jnp.sum(jnp.where(lane == row, center, 0.0), axis=1, keepdims=True)
    var = jnp.sum(
        jnp.where(lane == row, between, 0.0) + jnp.where(lane == row + 4, within, 0.0), axis=1, keepdims=True
    ) * (1.0 / D)
    rstd = lax.rsqrt(var + EPS)
    q, k, v = (
        rstd * (total[:, j * 128 : (j + 1) * 128] - mean * total[j : j + 1, 384:512]) for j in range(3)
    )
    cos, sin = cos_ref[...], sin_ref[...]
    q = (q * cos + pltpu.roll(q, 64, 1) * sin).astype(BF).astype(F32)
    k = (k * cos + pltpu.roll(k, 64, 1) * sin).astype(BF).astype(F32)
    v = v.astype(BF).astype(F32)
    place = lax.axis_index("seq")
    both = jnp.concatenate([q, q], axis=0)
    mine = (iota((8, 128), 0) >> 2) == (place & 1)
    q_ref[...] = jnp.broadcast_to(jnp.where(mine, both, 0.0).astype(BF)[None], (32, 8, 128))
    step = iota((4, 1), 0)
    scores = [
        jnp.where(step >= u, jnp.sum(q * k[u : u + 1], axis=1, keepdims=True) * SCALE, NEG) for u in range(4)
    ]
    top = jnp.maximum(jnp.maximum(scores[0], scores[1]), jnp.maximum(scores[2], scores[3]))
    weights = [jnp.where(step >= u, jnp.exp(scores[u] - top), 0.0) for u in range(4)]
    acc = sum(weights[u].astype(BF).astype(F32) * v[u : u + 1] for u in range(4))
    mass = weights[0] + weights[1] + weights[2] + weights[3]
    new_ref[0:4, :] = acc
    new_ref[4:8, :] = jnp.where(lane < 64, top, mass)


def attend_kernel(len_ref, q_ref, k_ref, v_ref, out_ref):
    group = pl.program_id(0)
    first = lax.axis_index("seq") * 512
    places = first + iota((8, 512), 1)
    row, lane = iota((8, 128), 0), iota((8, 128), 1)
    for j in range(4):
        valid = places < len_ref[group * 4 + j]
        q = jnp.concatenate([q_ref[2 * j], q_ref[2 * j + 1]], axis=1)
        scores = jnp.where(valid, mm(q, k_ref[j], NT) * SCALE, NEG)
        top = jnp.max(scores, axis=1, keepdims=True)
        weights = jnp.where(valid, jnp.exp(scores - top), 0.0)
        mass = jnp.sum(weights, axis=1, keepdims=True)
        acc = mm(weights.astype(BF), v_ref[j])
        stats = jnp.where(lane < 64, top, mass)
        out_ref[2 * j] = jnp.where(row < 4, acc[:, :128], pltpu.roll(stats, 4, 0))
        out_ref[2 * j + 1] = jnp.where(row < 4, pltpu.roll(acc[:, 128:], 4, 0), stats)


def combine_kernel(got_ref, new_ref, out_ref):
    row, lane = iota((8, 128), 0), iota((8, 128), 1)

    def parts(block):
        stats = pltpu.roll(block, 4, 0)
        other = pltpu.roll(stats, 64, 1)
        return jnp.where(lane < 64, stats, other), jnp.where(lane < 64, other, stats), block

    blocks = [parts(got_ref[i]) for i in range(32)] + [parts(new_ref[...])]
    top = functools.reduce(jnp.maximum, [b[0] for b in blocks])
    numer = jnp.zeros((8, 128), F32)
    denom = jnp.zeros((8, 128), F32)
    for block_top, mass, acc in blocks:
        factor = jnp.exp(block_top - top)
        numer = numer + factor * acc
        denom = denom + factor * mass
    attended = jnp.where(row < 4, numer / jnp.where(row < 4, denom, 1.0), 0.0)
    odd = (lax.axis_index("seq") >> 1) & 1
    placed = jnp.where(odd == 1, pltpu.roll(attended, 4, 0), attended)
    out_ref[...] = jnp.broadcast_to(placed.astype(BF)[None], (32, 8, 128))


def pack(v):
    return jnp.concatenate([v[0:32], v[32:64]], axis=1)


def unpack(v):
    return jnp.concatenate([v[:, 0:64], v[:, 64:128]], axis=0)


def out_proj_kernel(got_ref, w_ref, out_ref):
    got = got_ref[...].astype(F32).reshape(8, 2, 2, 8, 128)
    rows = got[:, 0] + got[:, 1]
    attended = jnp.concatenate([rows[:, 0].reshape(64, 128), rows[:, 1].reshape(64, 128)], axis=1).astype(BF)
    part = mm(w_ref[...], attended, NT)
    out_ref[...] = jnp.broadcast_to(pack(part)[None], (8, 32, 128))


def ffn_in_kernel(got_ref, x_ref, w_ref, branch_ref, out_ref):
    branch = unpack(jnp.sum(got_ref[...], axis=0))
    branch_ref[...] = mm(to_step_major(), branch.astype(BF), NT).astype(BF)
    eye = one_hot(iota((64, 64), 0) == iota((64, 64), 1))
    xt = mm(eye, mm(to_request_major(), x_ref[...]).astype(BF), NT)
    resid = xt + branch
    center = jnp.mean(resid, axis=0, keepdims=True)
    dev = resid - center
    spread = jnp.sum(dev * dev, axis=0, keepdims=True)
    zero = jnp.zeros((64, 64), F32)
    both = jnp.concatenate(
        [jnp.concatenate([dev, zero], axis=1), jnp.concatenate([zero, dev], axis=1)], axis=0
    ).astype(BF)
    weight = w_ref[...].reshape(128, 1024)
    prod = mm(weight, both, TN).astype(BF)
    out_ref[:, 0:16, :] = prod[0:512].reshape(32, 16, 128)
    out_ref[:, 16:32, :] = prod[512:1024].reshape(32, 16, 128)
    ones = jnp.ones((8, 64), BF)
    unit, slot = iota((32, 512), 1), iota((32, 512), 0)
    sums = jnp.zeros((32, 128), F32)
    for kind in range(2):
        cols = mm(ones, w_ref[kind])[0:1]
        for half in range(2):
            chosen = jnp.where((unit >> 4) == slot, cols[:, half * 512 : half * 512 + 512], 0.0).astype(BF)
            spot = one_hot(iota((512, 128), 1) == kind * 64 + half * 16 + (iota((512, 128), 0) & 15))
            sums = sums + mm(chosen, spot)
    row = iota((8, 128), 0)
    head = jnp.where(row == 0, split(center), jnp.where(row == 1, split(spread), 0.0))
    for s in range(32):
        out_ref[s, 32:40, :] = jnp.where(row == 2, sums[s : s + 1], head).astype(BF)


def hidden_kernel(got_ref, out_ref):
    total = jnp.sum(got_ref[:, 0:32, :].astype(F32), axis=0)
    extra = [got_ref[i, 32:40, :].astype(F32) for i in range(32)]
    center = jnp.concatenate([e[0:1] for e in extra], axis=0)
    center = center[:, 0:64] + center[:, 64:128]
    within = jnp.sum(jnp.concatenate([e[1:2] for e in extra], axis=0), axis=0, keepdims=True)
    within = within[:, 0:64] + within[:, 64:128]
    sums = jnp.concatenate([e[2:3] for e in extra], axis=0)
    mean = jnp.sum(center, axis=0, keepdims=True) * (1.0 / 32)
    shift = center - mean
    var = (within + 64.0 * jnp.sum(shift * shift, axis=0, keepdims=True)) * (1.0 / D)
    rstd = lax.rsqrt(var + EPS)
    fix = mm(sums.astype(BF), shift.astype(BF), TN)
    gate = rstd * (total[:, 0:64] + fix[0:32])
    up = rstd * (total[:, 64:128] + fix[64:96])
    hidden = gate / (1.0 + jnp.exp(-gate)) * up
    packed = jnp.concatenate([hidden[0:16], hidden[16:32]], axis=1).astype(BF)
    out_ref[...] = jnp.broadcast_to(packed[None], (32, 16, 128))


def ffn_out_kernel(got_ref, w_ref, out_ref):
    hidden = got_ref[...].reshape(512, 128)
    low = mm(w_ref[:, 0:512], hidden)
    high = mm(w_ref[:, 512:1024], hidden)
    part = low[:, 0:64] + high[:, 64:128]
    out_ref[...] = jnp.broadcast_to(pack(part)[None], (8, 32, 128))


def final_kernel(got_ref, out_ref):
    total = unpack(jnp.sum(got_ref[...], axis=0))
    out_ref[...] = mm(to_step_major(), total.astype(BF), NT).astype(BF)


def call(kernel, n_in, *outs):
    shapes = [jax.ShapeDtypeStruct(shape, dtype) for shape, dtype in outs]
    one = len(shapes) == 1
    return pl.pallas_call(
        kernel,
        out_shape=shapes[0] if one else shapes,
        in_specs=[VM] * n_in,
        out_specs=VM if one else [VM] * len(shapes),
        compiler_params=PARAMS,
    )


def exchange(values, axis):
    return lax.all_to_all(values, axis, 0, 0, tiled=False)


def per_device(
    tokens, attn_in_weight, attn_out_weight, ffn_in_weight, ffn_out_weight, cache_keys, cache_values, lengths
):
    x = tokens.reshape(64, 64)
    place = lax.axis_index("seq")
    freq = (10000.0 ** (-2.0 * np.arange(64) / HD)).astype(np.float32)
    freq = jnp.asarray(np.concatenate([freq, freq]))
    length = lax.dynamic_slice(lengths, (place // 2,), (1,))
    angles = (length + jnp.arange(4, dtype=jnp.int32)).astype(F32)[:, None] * freq[None, :]
    sign = jnp.asarray(np.concatenate([-np.ones(64, np.float32), np.ones(64, np.float32)]))
    cos, sin = jnp.cos(angles), jnp.sin(angles) * sign[None, :]

    got = exchange(call(qkv_kernel, 2, ((32, 4, 512), F32))(x, attn_in_weight), "seq")
    queries, new = call(rope_kernel, 3, ((32, 8, 128), BF), ((8, 128), F32))(got, cos, sin)
    queries = exchange(queries, "seq")
    blocks = pl.pallas_call(
        attend_kernel,
        out_shape=jax.ShapeDtypeStruct((32, 8, 128), F32),
        grid=(4,),
        in_specs=[
            pl.BlockSpec(memory_space=pltpu.SMEM),
            pl.BlockSpec((8, 8, 128), lambda g: (g, 0, 0)),
            pl.BlockSpec((4, 512, 256), lambda g: (g, 0, 0)),
            pl.BlockSpec((4, 512, 256), lambda g: (g, 0, 0)),
        ],
        out_specs=pl.BlockSpec((8, 8, 128), lambda g: (g, 0, 0)),
        compiler_params=pltpu.CompilerParams(vmem_limit_bytes=24 << 20),
    )(lengths, queries, cache_keys, cache_values)
    attended = exchange(call(combine_kernel, 2, ((32, 8, 128), BF))(exchange(blocks, "seq"), new), "seq")
    part = call(out_proj_kernel, 2, ((8, 32, 128), F32))(attended, attn_out_weight.T)
    branch, part = call(ffn_in_kernel, 3, ((64, 64), BF), ((32, 40, 128), BF))(
        exchange(part, "head"), x, ffn_in_weight
    )
    hidden = exchange(call(hidden_kernel, 1, ((32, 16, 128), BF))(exchange(part, "seq")), "seq")
    part = call(ffn_out_kernel, 2, ((8, 32, 128), F32))(hidden, ffn_out_weight.T)
    mlp = call(final_kernel, 1, ((64, 64), BF))(exchange(part, "head"))
    return branch.reshape(4, 16, 64), mlp.reshape(4, 16, 64)


def solution(mesh):
    in_specs = (
        P(None, None, "seq"),
        P(None, "seq", "head"),
        P("head", "seq"),
        P(None, "seq", "head"),
        P("head", "seq"),
        P(None, "seq", "head"),
        P(None, "seq", "head"),
        P(),
    )
    out_specs = (P(None, None, "seq"), P(None, None, "seq"))
    return jax.shard_map(per_device, mesh=mesh, in_specs=in_specs, out_specs=out_specs, check_vma=False)
```

```python
import functools

import numpy as np
import jax
import jax.numpy as jnp
from jax import lax
from jax.experimental import pallas as pl
from jax.experimental.pallas import tpu as pltpu
from jax.sharding import PartitionSpec as P

D = 2048
HD = 128
EPS = 1e-05
NEG = -1e30
SCALE = 1.0 / HD**0.5
F32 = jnp.float32
BF = jnp.bfloat16
NT = (((1,), (1,)), ((), ()))
TN = (((0,), (0,)), ((), ()))
VM = pl.BlockSpec(memory_space=pltpu.VMEM)
LONG = pl.CostEstimate(flops=1 << 40, bytes_accessed=1 << 40, transcendentals=0)
PARAMS = pltpu.CompilerParams(vmem_limit_bytes=16 << 20)


def iota(shape, axis):
    return lax.broadcasted_iota(jnp.int32, shape, axis)


def mm(a, b, dims=(((1,), (0,)), ((), ()))):
    return lax.dot_general(a, b, dims, preferred_element_type=F32)


def one_hot(cond):
    return jnp.where(cond, 1.0, 0.0).astype(BF)


def to_request_major():
    n, m = iota((64, 64), 0), iota((64, 64), 1)
    return one_hot(m == (n & 3) * 16 + (n >> 2))


def to_step_major():
    m, n = iota((64, 64), 0), iota((64, 64), 1)
    return one_hot(n == (m & 15) * 4 + (m >> 4))


def split(v):
    hi = v.astype(BF).astype(F32)
    return jnp.concatenate([hi, v - hi], axis=1)


def rotation(position, coarse_ref, fine_ref):
    lane = iota((4, 128), 1)
    spots = [position + t for t in range(4)]
    a = jnp.concatenate([coarse_ref[pl.ds(spot >> 7, 1), :] for spot in spots], axis=0)
    b = jnp.concatenate([fine_ref[pl.ds(spot & 127, 1), :] for spot in spots], axis=0)
    a_other, b_other = pltpu.roll(a, 64, 1), pltpu.roll(b, 64, 1)
    first = lane < 64
    side = a_other * jnp.where(first, b_other, b)
    both = a * jnp.where(first, b, b_other) + jnp.where(first, -side, side)
    other = pltpu.roll(both, 64, 1)
    return jnp.where(first, both, other), jnp.where(first, -other, both)


def qkv_kernel(x_hbm, w_hbm, out_ref, x_ref, w_ref, sems):
    copies = [
        pltpu.make_async_copy(x_hbm, x_ref, sems.at[0]),
        pltpu.make_async_copy(w_hbm, w_ref, sems.at[1]),
    ]
    for copy in copies:
        copy.start()
    copies[0].wait()
    xp = mm(to_request_major(), x_ref[...])
    center = jnp.mean(xp, axis=1, keepdims=True)
    dev = xp - center
    spread = jnp.sum(dev * dev, axis=1, keepdims=True)
    rows = jnp.concatenate([xp, jnp.ones((16, 64), F32)], axis=0).astype(BF)
    lane, row = iota((64, 128), 1), iota((64, 128), 0)
    placed = jnp.where(lane == (row & 3), center, 0.0) + jnp.where(lane == 4 + (row & 3), spread, 0.0)
    pick = jnp.where(iota((16, 64), 0) == (iota((16, 64), 1) >> 2), 1.0, 0.0)
    stats = lax.dot_general(
        pick, placed, (((1,), (0,)), ((), ())), precision=lax.Precision.HIGHEST, preferred_element_type=F32
    )
    copies[1].wait()
    for k in range(3):
        part = mm(rows, w_ref[k])
        for p in range(2):
            cols = part[:, p * 128 : (p + 1) * 128]
            for r in range(16):
                out_ref[2 * r + p, :, k * 128 : (k + 1) * 128] = cols[4 * r : 4 * r + 4]
                out_ref[2 * r + p, k : k + 1, 384:512] = cols[64:65]
    for r in range(16):
        for p in range(2):
            out_ref[2 * r + p, 3:4, 384:512] = stats[r : r + 1]


def rope_kernel(len_ref, got_ref, coarse_ref, fine_ref, q_ref, new_ref):
    total = jnp.sum(got_ref[...], axis=0)
    stats = jnp.concatenate([got_ref[i, 3:4, 384:512] for i in range(32)], axis=0)
    center = jnp.sum(stats, axis=0, keepdims=True) * (1.0 / 32)
    dev = stats - center
    between = jnp.sum(dev * dev, axis=0, keepdims=True) * 64.0
    within = jnp.sum(stats, axis=0, keepdims=True)
    lane, row = iota((4, 128), 1), iota((4, 128), 0)
    mean = jnp.sum(jnp.where(lane == row, center, 0.0), axis=1, keepdims=True)
    var = jnp.sum(
        jnp.where(lane == row, between, 0.0) + jnp.where(lane == row + 4, within, 0.0), axis=1, keepdims=True
    ) * (1.0 / D)
    rstd = lax.rsqrt(var + EPS)
    q, k, v = (
        rstd * (total[:, j * 128 : (j + 1) * 128] - mean * total[j : j + 1, 384:512]) for j in range(3)
    )
    cos, sin = rotation(len_ref[lax.axis_index("seq") >> 1], coarse_ref, fine_ref)
    q = (q * cos + pltpu.roll(q, 64, 1) * sin).astype(BF).astype(F32)
    k = (k * cos + pltpu.roll(k, 64, 1) * sin).astype(BF).astype(F32)
    v = v.astype(BF).astype(F32)
    place = lax.axis_index("seq")
    both = jnp.concatenate([q, q], axis=0)
    mine = (iota((8, 128), 0) >> 2) == (place & 1)
    q_ref[...] = jnp.broadcast_to(jnp.where(mine, both, 0.0).astype(BF)[None], (32, 8, 128))
    step = iota((4, 1), 0)
    scores = [
        jnp.where(step >= u, jnp.sum(q * k[u : u + 1], axis=1, keepdims=True) * SCALE, NEG) for u in range(4)
    ]
    top = jnp.maximum(jnp.maximum(scores[0], scores[1]), jnp.maximum(scores[2], scores[3]))
    weights = [jnp.where(step >= u, jnp.exp(scores[u] - top), 0.0) for u in range(4)]
    acc = sum(weights[u].astype(BF).astype(F32) * v[u : u + 1] for u in range(4))
    mass = weights[0] + weights[1] + weights[2] + weights[3]
    new_ref[0:4, :] = acc
    new_ref[4:8, :] = jnp.where(lane < 64, top, mass)


def attend_kernel(len_ref, q_ref, k_ref, v_ref, out_ref):
    first = lax.axis_index("seq") * 512
    places = first + iota((8, 512), 1)
    row, lane = iota((8, 128), 0), iota((8, 128), 1)
    lengths = len_ref[...]
    for r in range(16):
        valid = places < lengths[:, r : r + 1]
        q = jnp.concatenate([q_ref[2 * r], q_ref[2 * r + 1]], axis=1)
        scores = jnp.where(valid, mm(q, k_ref[r], NT) * SCALE, NEG)
        top = jnp.max(scores, axis=1, keepdims=True)
        weights = jnp.where(valid, jnp.exp(scores - top), 0.0)
        mass = jnp.sum(weights, axis=1, keepdims=True)
        acc = mm(weights.astype(BF), v_ref[r])
        stats = jnp.where(lane < 64, top, mass)
        out_ref[2 * r] = jnp.where(row < 4, acc[:, :128], pltpu.roll(stats, 4, 0))
        out_ref[2 * r + 1] = jnp.where(row < 4, pltpu.roll(acc[:, 128:], 4, 0), stats)


def combine_kernel(got_ref, new_ref, out_ref):
    row, lane = iota((8, 128), 0), iota((8, 128), 1)

    def parts(block):
        stats = pltpu.roll(block, 4, 0)
        other = pltpu.roll(stats, 64, 1)
        return jnp.where(lane < 64, stats, other), jnp.where(lane < 64, other, stats), block

    blocks = [parts(got_ref[i]) for i in range(32)] + [parts(new_ref[...])]
    top = functools.reduce(jnp.maximum, [b[0] for b in blocks])
    numer = jnp.zeros((8, 128), F32)
    denom = jnp.zeros((8, 128), F32)
    for block_top, mass, acc in blocks:
        factor = jnp.exp(block_top - top)
        numer = numer + factor * acc
        denom = denom + factor * mass
    attended = jnp.where(row < 4, numer / jnp.where(row < 4, denom, 1.0), 0.0)
    odd = (lax.axis_index("seq") >> 1) & 1
    placed = jnp.where(odd == 1, pltpu.roll(attended, 4, 0), attended)
    out_ref[...] = jnp.broadcast_to(placed.astype(BF)[None], (32, 8, 128))


def pack(v):
    return jnp.concatenate([v[0:32], v[32:64]], axis=1)


def unpack(v):
    return jnp.concatenate([v[:, 0:64], v[:, 64:128]], axis=0)


def out_proj_kernel(got_ref, w_ref, out_ref):
    got = got_ref[...].astype(F32).reshape(8, 2, 2, 8, 128)
    rows = got[:, 0] + got[:, 1]
    attended = jnp.concatenate([rows[:, 0].reshape(64, 128), rows[:, 1].reshape(64, 128)], axis=1).astype(BF)
    part = mm(w_ref[...], attended, NT)
    out_ref[...] = jnp.broadcast_to(pack(part)[None], (8, 32, 128))


def ffn_in_kernel(got_ref, x_ref, w_ref, branch_ref, out_ref):
    branch = unpack(jnp.sum(got_ref[...], axis=0))
    branch_ref[...] = mm(to_step_major(), branch.astype(BF), NT).astype(BF)
    eye = one_hot(iota((64, 64), 0) == iota((64, 64), 1))
    xt = mm(eye, mm(to_request_major(), x_ref[...]).astype(BF), NT)
    resid = xt + branch
    center = jnp.mean(resid, axis=0, keepdims=True)
    dev = resid - center
    spread = jnp.sum(dev * dev, axis=0, keepdims=True)
    zero = jnp.zeros((64, 64), F32)
    both = jnp.concatenate(
        [jnp.concatenate([dev, zero], axis=1), jnp.concatenate([zero, dev], axis=1)], axis=0
    ).astype(BF)
    weight = w_ref[...].reshape(128, 1024)
    prod = mm(weight, both, TN).astype(BF)
    out_ref[:, 0:16, :] = prod[0:512].reshape(32, 16, 128)
    out_ref[:, 16:32, :] = prod[512:1024].reshape(32, 16, 128)
    ones = jnp.ones((8, 64), BF)
    unit, slot = iota((32, 512), 1), iota((32, 512), 0)
    sums = jnp.zeros((32, 128), F32)
    for kind in range(2):
        cols = mm(ones, w_ref[kind])[0:1]
        for half in range(2):
            chosen = jnp.where((unit >> 4) == slot, cols[:, half * 512 : half * 512 + 512], 0.0).astype(BF)
            spot = one_hot(iota((512, 128), 1) == kind * 64 + half * 16 + (iota((512, 128), 0) & 15))
            sums = sums + mm(chosen, spot)
    row = iota((8, 128), 0)
    head = jnp.where(row == 0, split(center), jnp.where(row == 1, split(spread), 0.0))
    for s in range(32):
        out_ref[s, 32:40, :] = jnp.where(row == 2, sums[s : s + 1], head).astype(BF)


def hidden_kernel(got_ref, out_ref):
    total = jnp.sum(got_ref[:, 0:32, :].astype(F32), axis=0)
    extra = [got_ref[i, 32:40, :].astype(F32) for i in range(32)]
    center = jnp.concatenate([e[0:1] for e in extra], axis=0)
    center = center[:, 0:64] + center[:, 64:128]
    within = jnp.sum(jnp.concatenate([e[1:2] for e in extra], axis=0), axis=0, keepdims=True)
    within = within[:, 0:64] + within[:, 64:128]
    sums = jnp.concatenate([e[2:3] for e in extra], axis=0)
    mean = jnp.sum(center, axis=0, keepdims=True) * (1.0 / 32)
    shift = center - mean
    var = (within + 64.0 * jnp.sum(shift * shift, axis=0, keepdims=True)) * (1.0 / D)
    rstd = lax.rsqrt(var + EPS)
    fix = mm(sums.astype(BF), shift.astype(BF), TN)
    gate = rstd * (total[:, 0:64] + fix[0:32])
    up = rstd * (total[:, 64:128] + fix[64:96])
    hidden = gate / (1.0 + jnp.exp(-gate)) * up
    packed = jnp.concatenate([hidden[0:16], hidden[16:32]], axis=1).astype(BF)
    out_ref[...] = jnp.broadcast_to(packed[None], (32, 16, 128))


def ffn_out_kernel(got_ref, w_ref, out_ref):
    hidden = got_ref[...].reshape(512, 128)
    low = mm(w_ref[:, 0:512], hidden)
    high = mm(w_ref[:, 512:1024], hidden)
    part = low[:, 0:64] + high[:, 64:128]
    out_ref[...] = jnp.broadcast_to(pack(part)[None], (8, 32, 128))


def final_kernel(got_ref, out_ref):
    total = unpack(jnp.sum(got_ref[...], axis=0))
    out_ref[...] = mm(to_step_major(), total.astype(BF), NT).astype(BF)


def call(kernel, n_in, *outs):
    shapes = [jax.ShapeDtypeStruct(shape, dtype) for shape, dtype in outs]
    one = len(shapes) == 1
    return pl.pallas_call(
        kernel,
        out_shape=shapes[0] if one else shapes,
        in_specs=[VM] * n_in,
        out_specs=VM if one else [VM] * len(shapes),
        compiler_params=PARAMS,
    )


def exchange(values, axis):
    return lax.all_to_all(values, axis, 0, 0, tiled=False)


def angle_tables():
    freq = 10000.0 ** (-2.0 * np.arange(64) / HD)
    tables = []
    for positions in (np.arange(136) * 128, np.arange(128)):
        angles = positions[:, None] * freq[None, :]
        tables.append(np.concatenate([np.cos(angles), np.sin(angles)], axis=1).astype(np.float32))
    return tables


def per_device(
    tokens, attn_in_weight, attn_out_weight, ffn_in_weight, ffn_out_weight, cache_keys, cache_values, lengths
):
    x = tokens.reshape(64, 64)
    coarse, fine = (jnp.asarray(table) for table in angle_tables())
    part = pl.pallas_call(
        qkv_kernel,
        out_shape=jax.ShapeDtypeStruct((32, 4, 512), F32),
        in_specs=[pl.BlockSpec(memory_space=pl.ANY)] * 2,
        out_specs=VM,
        scratch_shapes=[
            pltpu.VMEM((64, 64), BF),
            pltpu.VMEM((3, 64, 256), BF),
            pltpu.SemaphoreType.DMA((2,)),
        ],
        compiler_params=pltpu.CompilerParams(vmem_limit_bytes=60 << 20),
        cost_estimate=LONG,
    )(x, attn_in_weight)
    got = exchange(part, "seq")
    queries, new = pl.pallas_call(
        rope_kernel,
        out_shape=[jax.ShapeDtypeStruct((32, 8, 128), BF), jax.ShapeDtypeStruct((8, 128), F32)],
        in_specs=[pl.BlockSpec(memory_space=pltpu.SMEM)] + [VM] * 3,
        out_specs=[VM] * 2,
        compiler_params=PARAMS,
        cost_estimate=LONG,
    )(lengths, got, coarse, fine)
    queries = exchange(queries, "seq")
    blocks = call(attend_kernel, 4, ((32, 8, 128), F32))(lengths.reshape(1, 16), queries, cache_keys, cache_values)
    attended = exchange(call(combine_kernel, 2, ((32, 8, 128), BF))(exchange(blocks, "seq"), new), "seq")
    part = call(out_proj_kernel, 2, ((8, 32, 128), F32))(attended, attn_out_weight.T)
    branch, part = call(ffn_in_kernel, 3, ((64, 64), BF), ((32, 40, 128), BF))(
        exchange(part, "head"), x, ffn_in_weight
    )
    hidden = exchange(call(hidden_kernel, 1, ((32, 16, 128), BF))(exchange(part, "seq")), "seq")
    part = call(ffn_out_kernel, 2, ((8, 32, 128), F32))(hidden, ffn_out_weight.T)
    mlp = call(final_kernel, 1, ((64, 64), BF))(exchange(part, "head"))
    return branch.reshape(4, 16, 64), mlp.reshape(4, 16, 64)


def solution(mesh):
    in_specs = (
        P(None, None, "seq"),
        P(None, "seq", "head"),
        P("head", "seq"),
        P(None, "seq", "head"),
        P("head", "seq"),
        P(None, "seq", "head"),
        P(None, "seq", "head"),
        P(),
    )
    out_specs = (P(None, None, "seq"), P(None, None, "seq"))
    return jax.shard_map(per_device, mesh=mesh, in_specs=in_specs, out_specs=out_specs, check_vma=False)
```

```python
import functools

import numpy as np
import jax
import jax.numpy as jnp
from jax import lax
from jax.experimental import pallas as pl
from jax.experimental.pallas import tpu as pltpu
from jax.sharding import PartitionSpec as P

D = 2048
HD = 128
EPS = 1e-05
NEG = -1e30
SCALE = 1.0 / HD**0.5
F32 = jnp.float32
BF = jnp.bfloat16
NT = (((1,), (1,)), ((), ()))
TN = (((0,), (0,)), ((), ()))
VM = pl.BlockSpec(memory_space=pltpu.VMEM)
LONG = pl.CostEstimate(flops=1 << 40, bytes_accessed=1 << 40, transcendentals=0)
PARAMS = pltpu.CompilerParams(vmem_limit_bytes=16 << 20)


def iota(shape, axis):
    return lax.broadcasted_iota(jnp.int32, shape, axis)


def mm(a, b, dims=(((1,), (0,)), ((), ()))):
    return lax.dot_general(a, b, dims, preferred_element_type=F32)


def one_hot(cond):
    return jnp.where(cond, 1.0, 0.0).astype(BF)


def to_request_major():
    n, m = iota((64, 64), 0), iota((64, 64), 1)
    return one_hot(m == (n & 3) * 16 + (n >> 2))


def to_step_major():
    m, n = iota((64, 64), 0), iota((64, 64), 1)
    return one_hot(n == (m & 15) * 4 + (m >> 4))


def split(v):
    hi = v.astype(BF).astype(F32)
    return jnp.concatenate([hi, v - hi], axis=1)


def rotation(position, coarse_ref, fine_ref):
    lane = iota((4, 128), 1)
    spots = [position + t for t in range(4)]
    a = jnp.concatenate([coarse_ref[pl.ds(spot >> 7, 1), :] for spot in spots], axis=0)
    b = jnp.concatenate([fine_ref[pl.ds(spot & 127, 1), :] for spot in spots], axis=0)
    a_other, b_other = pltpu.roll(a, 64, 1), pltpu.roll(b, 64, 1)
    first = lane < 64
    side = a_other * jnp.where(first, b_other, b)
    both = a * jnp.where(first, b, b_other) + jnp.where(first, -side, side)
    other = pltpu.roll(both, 64, 1)
    return jnp.where(first, both, other), jnp.where(first, -other, both)


def qkv_kernel(x_hbm, w_hbm, out_ref, x_ref, w_ref, sems):
    copies = [
        pltpu.make_async_copy(x_hbm, x_ref, sems.at[0]),
        pltpu.make_async_copy(w_hbm, w_ref, sems.at[1]),
    ]
    for copy in copies:
        copy.start()
    copies[0].wait()
    xp = mm(to_request_major(), x_ref[...])
    center = jnp.mean(xp, axis=1, keepdims=True)
    dev = xp - center
    spread = jnp.sum(dev * dev, axis=1, keepdims=True)
    rows = jnp.concatenate([xp, jnp.ones((16, 64), F32)], axis=0).astype(BF)
    lane, row = iota((64, 128), 1), iota((64, 128), 0)
    placed = jnp.where(lane == (row & 3), center, 0.0) + jnp.where(lane == 4 + (row & 3), spread, 0.0)
    pick = jnp.where(iota((16, 64), 0) == (iota((16, 64), 1) >> 2), 1.0, 0.0)
    stats = lax.dot_general(
        pick, placed, (((1,), (0,)), ((), ())), precision=lax.Precision.HIGHEST, preferred_element_type=F32
    )
    copies[1].wait()
    for k in range(3):
        part = mm(rows, w_ref[k])
        for p in range(2):
            cols = part[:, p * 128 : (p + 1) * 128]
            for r in range(16):
                out_ref[2 * r + p, :, k * 128 : (k + 1) * 128] = cols[4 * r : 4 * r + 4]
                out_ref[2 * r + p, k : k + 1, 384:512] = cols[64:65]
    for r in range(16):
        for p in range(2):
            out_ref[2 * r + p, 3:4, 384:512] = stats[r : r + 1]


def rope_kernel(len_ref, got_ref, coarse_ref, fine_ref, q_ref, new_ref):
    total = jnp.sum(got_ref[...], axis=0)
    stats = jnp.concatenate([got_ref[i, 3:4, 384:512] for i in range(32)], axis=0)
    center = jnp.sum(stats, axis=0, keepdims=True) * (1.0 / 32)
    dev = stats - center
    between = jnp.sum(dev * dev, axis=0, keepdims=True) * 64.0
    within = jnp.sum(stats, axis=0, keepdims=True)
    lane, row = iota((4, 128), 1), iota((4, 128), 0)
    mean = jnp.sum(jnp.where(lane == row, center, 0.0), axis=1, keepdims=True)
    var = jnp.sum(
        jnp.where(lane == row, between, 0.0) + jnp.where(lane == row + 4, within, 0.0), axis=1, keepdims=True
    ) * (1.0 / D)
    rstd = lax.rsqrt(var + EPS)
    q, k, v = (
        rstd * (total[:, j * 128 : (j + 1) * 128] - mean * total[j : j + 1, 384:512]) for j in range(3)
    )
    cos, sin = rotation(len_ref[lax.axis_index("seq") >> 1], coarse_ref, fine_ref)
    q = (q * cos + pltpu.roll(q, 64, 1) * sin).astype(BF).astype(F32)
    k = (k * cos + pltpu.roll(k, 64, 1) * sin).astype(BF).astype(F32)
    v = v.astype(BF).astype(F32)
    place = lax.axis_index("seq")
    both = jnp.concatenate([q, q], axis=0)
    mine = (iota((8, 128), 0) >> 2) == (place & 1)
    q_ref[...] = jnp.broadcast_to(jnp.where(mine, both, 0.0).astype(BF)[None], (32, 8, 128))
    step = iota((4, 1), 0)
    scores = [
        jnp.where(step >= u, jnp.sum(q * k[u : u + 1], axis=1, keepdims=True) * SCALE, NEG) for u in range(4)
    ]
    top = jnp.maximum(jnp.maximum(scores[0], scores[1]), jnp.maximum(scores[2], scores[3]))
    weights = [jnp.where(step >= u, jnp.exp(scores[u] - top), 0.0) for u in range(4)]
    acc = sum(weights[u].astype(BF).astype(F32) * v[u : u + 1] for u in range(4))
    mass = weights[0] + weights[1] + weights[2] + weights[3]
    new_ref[0:4, :] = acc
    new_ref[4:8, :] = jnp.where(lane < 64, top, mass)


def attend_kernel(len_ref, q_ref, k_ref, v_ref, out_ref, score_ref, weight_ref, stat_ref):
    first = lax.axis_index("seq") * 512
    places = first + iota((8, 512), 1)
    row, lane = iota((8, 128), 0), iota((8, 128), 1)
    lengths = len_ref[...]
    for r in range(16):
        q = jnp.concatenate([q_ref[2 * r], q_ref[2 * r + 1]], axis=1)
        score_ref[r] = mm(q, k_ref[r], NT) * SCALE
    for r in range(16):
        valid = places < lengths[:, r : r + 1]
        scores = jnp.where(valid, score_ref[r], NEG)
        top = jnp.max(scores, axis=1, keepdims=True)
        weights = jnp.where(valid, jnp.exp(scores - top), 0.0)
        mass = jnp.sum(weights, axis=1, keepdims=True)
        weight_ref[r] = weights.astype(BF)
        stat_ref[r] = jnp.where(lane < 64, top, mass)
    for r in range(16):
        acc = mm(weight_ref[r], v_ref[r])
        stats = stat_ref[r]
        out_ref[2 * r] = jnp.where(row < 4, acc[:, :128], pltpu.roll(stats, 4, 0))
        out_ref[2 * r + 1] = jnp.where(row < 4, pltpu.roll(acc[:, 128:], 4, 0), stats)


def combine_kernel(got_ref, new_ref, out_ref):
    row, lane = iota((8, 128), 0), iota((8, 128), 1)

    def parts(block):
        stats = pltpu.roll(block, 4, 0)
        other = pltpu.roll(stats, 64, 1)
        return jnp.where(lane < 64, stats, other), jnp.where(lane < 64, other, stats), block

    blocks = [parts(got_ref[i]) for i in range(32)] + [parts(new_ref[...])]
    top = functools.reduce(jnp.maximum, [b[0] for b in blocks])
    numer = jnp.zeros((8, 128), F32)
    denom = jnp.zeros((8, 128), F32)
    for block_top, mass, acc in blocks:
        factor = jnp.exp(block_top - top)
        numer = numer + factor * acc
        denom = denom + factor * mass
    attended = jnp.where(row < 4, numer / jnp.where(row < 4, denom, 1.0), 0.0)
    odd = (lax.axis_index("seq") >> 1) & 1
    placed = jnp.where(odd == 1, pltpu.roll(attended, 4, 0), attended)
    out_ref[...] = jnp.broadcast_to(placed.astype(BF)[None], (32, 8, 128))


def pack(v):
    return jnp.concatenate([v[0:32], v[32:64]], axis=1)


def unpack(v):
    return jnp.concatenate([v[:, 0:64], v[:, 64:128]], axis=0)


def out_proj_kernel(got_ref, w_ref, out_ref):
    got = got_ref[...].astype(F32).reshape(8, 2, 2, 8, 128)
    rows = got[:, 0] + got[:, 1]
    attended = jnp.concatenate([rows[:, 0].reshape(64, 128), rows[:, 1].reshape(64, 128)], axis=1).astype(BF)
    part = mm(w_ref[...], attended, NT)
    out_ref[...] = jnp.broadcast_to(pack(part).astype(BF)[None], (8, 32, 128))


def ffn_in_kernel(got_ref, x_ref, w_ref, branch_ref, out_ref):
    branch = unpack(jnp.sum(got_ref[...].astype(F32), axis=0))
    branch_ref[...] = mm(to_step_major(), branch.astype(BF), NT).astype(BF)
    eye = one_hot(iota((64, 64), 0) == iota((64, 64), 1))
    xt = mm(eye, mm(to_request_major(), x_ref[...]).astype(BF), NT)
    resid = xt + branch
    center = jnp.mean(resid, axis=0, keepdims=True)
    dev = resid - center
    spread = jnp.sum(dev * dev, axis=0, keepdims=True)
    zero = jnp.zeros((64, 64), F32)
    both = jnp.concatenate(
        [jnp.concatenate([dev, zero], axis=1), jnp.concatenate([zero, dev], axis=1)], axis=0
    ).astype(BF)
    weight = w_ref[...].reshape(128, 1024)
    prod = mm(weight, both, TN).astype(BF)
    out_ref[:, 0:16, :] = prod[0:512].reshape(32, 16, 128)
    out_ref[:, 16:32, :] = prod[512:1024].reshape(32, 16, 128)
    ones = jnp.ones((8, 64), BF)
    unit, slot = iota((32, 512), 1), iota((32, 512), 0)
    sums = jnp.zeros((32, 128), F32)
    for kind in range(2):
        cols = mm(ones, w_ref[kind])[0:1]
        for half in range(2):
            chosen = jnp.where((unit >> 4) == slot, cols[:, half * 512 : half * 512 + 512], 0.0).astype(BF)
            spot = one_hot(iota((512, 128), 1) == kind * 64 + half * 16 + (iota((512, 128), 0) & 15))
            sums = sums + mm(chosen, spot)
    row = iota((8, 128), 0)
    head = jnp.where(row == 0, split(center), jnp.where(row == 1, split(spread), 0.0))
    for s in range(32):
        out_ref[s, 32:40, :] = jnp.where(row == 2, sums[s : s + 1], head).astype(BF)


def hidden_kernel(got_ref, out_ref):
    total = jnp.sum(got_ref[:, 0:32, :].astype(F32), axis=0)
    extra = [got_ref[i, 32:40, :].astype(F32) for i in range(32)]
    center = jnp.concatenate([e[0:1] for e in extra], axis=0)
    center = center[:, 0:64] + center[:, 64:128]
    within = jnp.sum(jnp.concatenate([e[1:2] for e in extra], axis=0), axis=0, keepdims=True)
    within = within[:, 0:64] + within[:, 64:128]
    sums = jnp.concatenate([e[2:3] for e in extra], axis=0)
    mean = jnp.sum(center, axis=0, keepdims=True) * (1.0 / 32)
    shift = center - mean
    var = (within + 64.0 * jnp.sum(shift * shift, axis=0, keepdims=True)) * (1.0 / D)
    rstd = lax.rsqrt(var + EPS)
    fix = mm(sums.astype(BF), shift.astype(BF), TN)
    gate = rstd * (total[:, 0:64] + fix[0:32])
    up = rstd * (total[:, 64:128] + fix[64:96])
    hidden = gate / (1.0 + jnp.exp(-gate)) * up
    packed = jnp.concatenate([hidden[0:16], hidden[16:32]], axis=1).astype(BF)
    out_ref[...] = jnp.broadcast_to(packed[None], (32, 16, 128))


def ffn_out_kernel(got_ref, w_ref, out_ref):
    hidden = got_ref[...].reshape(512, 128)
    low = mm(w_ref[:, 0:512], hidden)
    high = mm(w_ref[:, 512:1024], hidden)
    part = low[:, 0:64] + high[:, 64:128]
    out_ref[...] = jnp.broadcast_to(pack(part).astype(BF)[None], (8, 32, 128))


def final_kernel(got_ref, out_ref):
    total = unpack(jnp.sum(got_ref[...].astype(F32), axis=0))
    out_ref[...] = mm(to_step_major(), total.astype(BF), NT).astype(BF)


def call(kernel, n_in, *outs, scratch=()):
    shapes = [jax.ShapeDtypeStruct(shape, dtype) for shape, dtype in outs]
    one = len(shapes) == 1
    return pl.pallas_call(
        kernel,
        out_shape=shapes[0] if one else shapes,
        in_specs=[VM] * n_in,
        out_specs=VM if one else [VM] * len(shapes),
        scratch_shapes=scratch,
        compiler_params=PARAMS,
    )


def exchange(values, axis):
    return lax.all_to_all(values, axis, 0, 0, tiled=False)


def angle_tables():
    freq = 10000.0 ** (-2.0 * np.arange(64) / HD)
    tables = []
    for positions in (np.arange(136) * 128, np.arange(128)):
        angles = positions[:, None] * freq[None, :]
        tables.append(np.concatenate([np.cos(angles), np.sin(angles)], axis=1).astype(np.float32))
    return tables


def per_device(
    tokens, attn_in_weight, attn_out_weight, ffn_in_weight, ffn_out_weight, cache_keys, cache_values, lengths
):
    x = tokens.reshape(64, 64)
    coarse, fine = (jnp.asarray(table) for table in angle_tables())
    part = pl.pallas_call(
        qkv_kernel,
        out_shape=jax.ShapeDtypeStruct((32, 4, 512), F32),
        in_specs=[pl.BlockSpec(memory_space=pltpu.HBM)] * 2,
        out_specs=VM,
        scratch_shapes=[
            pltpu.VMEM((64, 64), BF),
            pltpu.VMEM((3, 64, 256), BF),
            pltpu.SemaphoreType.DMA((2,)),
        ],
        compiler_params=PARAMS,
        cost_estimate=LONG,
    )(
        pltpu.with_memory_space_constraint(x, pltpu.HBM),
        pltpu.with_memory_space_constraint(attn_in_weight, pltpu.HBM),
    )
    got = exchange(part, "seq")
    queries, new = pl.pallas_call(
        rope_kernel,
        out_shape=[jax.ShapeDtypeStruct((32, 8, 128), BF), jax.ShapeDtypeStruct((8, 128), F32)],
        in_specs=[pl.BlockSpec(memory_space=pltpu.SMEM)] + [VM] * 3,
        out_specs=[VM] * 2,
        compiler_params=PARAMS,
        cost_estimate=LONG,
    )(lengths, got, coarse, fine)
    queries = exchange(queries, "seq")
    scratch = [pltpu.VMEM((16, 8, 512), F32), pltpu.VMEM((16, 8, 512), BF), pltpu.VMEM((16, 8, 128), F32)]
    blocks = call(attend_kernel, 4, ((32, 8, 128), F32), scratch=scratch)(lengths.reshape(1, 16), queries, cache_keys, cache_values)
    attended = exchange(call(combine_kernel, 2, ((32, 8, 128), BF))(exchange(blocks, "seq"), new), "seq")
    part = call(out_proj_kernel, 2, ((8, 32, 128), BF))(attended, attn_out_weight.T)
    branch, part = call(ffn_in_kernel, 3, ((64, 64), BF), ((32, 40, 128), BF))(
        exchange(part, "head"), x, ffn_in_weight
    )
    hidden = exchange(call(hidden_kernel, 1, ((32, 16, 128), BF))(exchange(part, "seq")), "seq")
    part = call(ffn_out_kernel, 2, ((8, 32, 128), BF))(hidden, ffn_out_weight.T)
    mlp = call(final_kernel, 1, ((64, 64), BF))(exchange(part, "head"))
    return branch.reshape(4, 16, 64), mlp.reshape(4, 16, 64)


def solution(mesh):
    in_specs = (
        P(None, None, "seq"),
        P(None, "seq", "head"),
        P("head", "seq"),
        P(None, "seq", "head"),
        P("head", "seq"),
        P(None, "seq", "head"),
        P(None, "seq", "head"),
        P(),
    )
    out_specs = (P(None, None, "seq"), P(None, None, "seq"))
    return jax.shard_map(per_device, mesh=mesh, in_specs=in_specs, out_specs=out_specs, check_vma=False)
```
